256 devices in a mesh: tm: 16 (over y, x), space: 2 (over core), head: 8 (over z).
Axes of the slice: x: 4, y: 4, z: 8, core: 2. Of those that a mesh axis runs over, the one named last changes fastest.
Arguments:
- query: bfloat16 [16, 8, 80, 5120], P('tm', 'space', None, 'head'), may hold values from -5 to 5
- key: bfloat16 [16, 8, 80, 5120], P('tm', 'space', None, 'head'), may hold values from -5 to 5
- value: bfloat16 [16, 8, 80, 5120], P('tm', 'space', None, 'head'), may hold values from -6 to 6
- window: int32 [16, 16], replicated, may hold values from -1 to 4, as said below
- out_weight: bfloat16 [5120, 5120], P('head'), may hold values from -0.078125 to 0.078125
Outputs:
- projected: bfloat16 [16, 8, 80, 5120], P('tm', 'space', None, 'head')
The draws below stay inside these ranges and needn't reach their ends.
Inputs may be any that keep to these rules, and one draw needn't show every extreme that they name: window[f, f] = 4 for every frame f.
All inputs are finite; a program needn't handle non-finite values.
Results may differ from the reference program's by a relative error of at most 0.023.
Values may be sent and summed in bfloat16 or wider, within the bound.
A program may use at most 128 MiB of HBM per device.

```python
import math
import jax
import jax.numpy as jnp
from jax import lax

HD = 128
D = 5120
WIDTH = 80
HALO = 4
FRAMES = 16
ROWS = 8


def drawn_pair(key):
    base_stream = jax.random.fold_in(key, 11)
    query_stream, key_stream = jax.random.split(base_stream, 2)
    shape = (FRAMES, ROWS, WIDTH, D)
    query_part = jnp.clip(jax.random.normal(query_stream, shape, jnp.float32), -5.0, 5.0)
    key_part = jnp.clip(jax.random.normal(key_stream, shape, jnp.float32), -5.0, 5.0)
    return (query_part, key_part)


def draw_query(key, part):
    return drawn_pair(key)[0].astype(jnp.bfloat16)


def draw_key(key, part):
    return drawn_pair(key)[1].astype(jnp.bfloat16)


def draw_window(key, part):
    stream = jax.random.fold_in(key, 23)
    raw_width = jax.random.randint(stream, (FRAMES, FRAMES), -1, HALO + 1)
    first = jnp.arange(FRAMES, dtype=jnp.int32)[:, None]
    second = jnp.arange(FRAMES, dtype=jnp.int32)[None, :]
    distance = jnp.abs(first - second)
    ceiling = HALO - (HALO + 1) * distance // FRAMES
    banded = jnp.maximum(jnp.minimum(raw_width, ceiling), -1)
    return jnp.where(distance == 0, HALO, banded).astype(jnp.int32)


def block_levels(rng, shape, shards, smallest, largest):
    level = 1.0
    for position, blocks in shards:
        draws = jax.random.uniform(jax.random.fold_in(jax.random.fold_in(rng, 6), position), (blocks,), jnp.float32, smallest / len(shards), largest / len(shards))
        level = level * jnp.repeat(jnp.exp(draws), shape[position] // blocks).reshape((-1,) + (1,) * (len(shape) - 1 - position))
    return level


def bell_draw(stream_key, dims, scale, limit, shards=(), held_as=jnp.bfloat16):
    drawn = scale * jax.random.normal(stream_key, dims, jnp.float32)
    if shards:
        drawn = drawn * block_levels(stream_key, dims, shards, -0.22, 0.18)
    return jnp.clip(drawn, -limit, limit).astype(held_as)


def setup_inputs(seed: int = 0) -> dict:
    keys = jax.random.split(jax.random.key(seed), 6)
    return {
        "query": draw_query(jax.random.fold_in(keys[5], 71), 0),
        "key": draw_key(jax.random.fold_in(keys[5], 71), 0),
        "value": bell_draw(keys[2], (FRAMES, ROWS, WIDTH, D), 1.0, 6.0, ((0, 16), (1, 2), (3, 8))),
        "window": draw_window(jax.random.fold_in(keys[5], 71), 0),
        "out_weight": bell_draw(keys[4], (D, D), D ** -0.5, 0.078125, ((0, 8),)),
    }


NEG_FILL = -1e+30

def reference(query, key, value, window, out_weight):
    frames, rows, width, feats = query.shape
    heads = feats // HD
    tokens = frames * rows * width
    per_frame = rows * width
    all_keys = key.reshape(tokens, heads, HD).transpose(1, 0, 2)
    all_values = value.reshape(tokens, heads, HD).transpose(1, 0, 2)
    all_queries = query.reshape(frames, per_frame, heads, HD).transpose(0, 2, 1, 3)
    row_ids = jnp.arange(rows, dtype=jnp.int32)
    distance = jnp.abs(row_ids[:, None] - row_ids[None, :])
    scale = 1.0 / math.sqrt(HD)

    def attend(index):
        frame = index // heads
        head = index % heads
        frame_query = lax.dynamic_index_in_dim(lax.dynamic_index_in_dim(all_queries, frame, 0, False), head, 0, False)
        head_keys = lax.dynamic_index_in_dim(all_keys, head, 0, False)
        head_values = lax.dynamic_index_in_dim(all_values, head, 0, False)
        widths = lax.dynamic_index_in_dim(window, frame, 0, False)
        inside = (widths[None, :, None] >= 0) & (distance[:, None, :] <= widths[None, :, None])
        mask = jnp.broadcast_to(inside[:, None, :, :, None], (rows, width, frames, rows, width)).reshape(per_frame, tokens)
        scores = jnp.dot(frame_query, head_keys.T, preferred_element_type=jnp.float32) * scale
        top = lax.optimization_barrier(jnp.max(jnp.where(mask, scores, NEG_FILL), axis=-1))
        weights = jnp.where(mask, jnp.exp(scores - top[:, None]), 0.0)
        summed = jnp.dot(weights.astype(jnp.bfloat16), head_values, preferred_element_type=jnp.float32)
        return summed / lax.optimization_barrier(jnp.sum(weights, axis=-1))[:, None]
    outputs = lax.map(attend, jnp.arange(frames * heads, dtype=jnp.int32))
    attended = outputs.reshape(frames, heads, per_frame, HD).transpose(0, 2, 1, 3).reshape(tokens, feats).astype(jnp.bfloat16)
    projected = jnp.dot(attended, out_weight, preferred_element_type=jnp.float32).astype(jnp.bfloat16)
    return projected.reshape(frames, rows, width, feats)
```

```python
import functools
import math

import jax
import jax.numpy as jnp
from jax import lax
from jax.experimental import pallas as pl
from jax.experimental.pallas import tpu as pltpu
from jax.sharding import PartitionSpec as P

HD = 128
SIDE = 4
NEG_FILL = -1e30
MAX_START = -1e20
MESH = pl.DeviceIdType.MESH

GRAY = (0, 1, 3, 2)
MAIN_ORDER = (
    (0, 0), (0, 1), (-1, 0), (0, 2), (1, 0), (0, 3), (-1, 1), (1, 1),
    (-1, 2), (1, 2), (2, 0), (2, 1), (-1, 3), (1, 3), (2, 2), (2, 3),
)
LAST_ORDER = (
    (0, 0), (0, 1), (0, 2), (0, 3), (-1, 0), (1, 0), (-1, 1), (1, 1),
    (-1, 2), (1, 2), (2, 0), (2, 1), (-1, 3), (1, 3), (2, 2), (2, 3),
)
PLUS = (0, 2)
MINUS = (1, 3)
N_SENDS = 96


def pick(index, values):
    out = values[0]
    for position, value in enumerate(values[1:], 1):
        out = jnp.where(index == position, value, out)
    return out


def greet(partners):
    barrier = pltpu.get_barrier_semaphore()
    for partner in partners:
        pl.semaphore_signal(barrier, inc=1, device_id=partner, device_id_type=MESH)
    pl.semaphore_wait(barrier, len(partners))


def attend_kernel(
    window, q_ref, k_ref, v_ref, o_ref,
    kv_main, kv_last, q_main, far, s_even, s_odd, run_max, run_sum, run_acc,
    send_sem, main_sem, last_sem, main_pair_sem, last_pair_sem, q_sem, local_sem,
):
    scale = math.log2(math.e) / math.sqrt(HD)
    tm, core = lax.axis_index("tm"), lax.axis_index("space")
    y, x = tm // SIDE, tm % SIDE
    frame = {
        (dy, dx): ((y + dy) % SIDE) * SIDE + (x + dx) % SIDE for dy in range(4) for dx in range(4)
    }
    up, down, across_y = ({"tm": frame[(d, 0)]} for d in (1, 3, 2))
    right, left, across_x = ({"tm": frame[(0, d)]} for d in (1, 3, 2))
    pair = {"space": 1 - core}
    greet([up, down, across_y, right, left, across_x, pair])

    counts = {"piece": 0, "block": 0}
    block = 320
    tokens = k_ref.shape[0]

    def send(src, dst, recv_sem, device, kind="piece"):
        slot = counts["piece"] if kind == "piece" else N_SENDS - 1 - counts["block"]
        counts[kind] += 1
        pltpu.make_async_remote_copy(
            src_ref=src, dst_ref=dst, send_sem=send_sem.at[slot], recv_sem=recv_sem,
            device_id=device, device_id_type=MESH,
        ).start()

    def head_of(ref, head):
        return ref.at[:, pl.ds(pl.multiple_of(head * HD, HD), HD)]

    mine = frame[(0, 0)]
    local = [
        pltpu.make_async_copy(head_of(q_ref, x), q_main.at[x], local_sem.at[0]),
        pltpu.make_async_copy(head_of(k_ref, x), kv_main.at[mine, core, 0], local_sem.at[1]),
        pltpu.make_async_copy(head_of(v_ref, x), kv_main.at[mine, core, 1], local_sem.at[2]),
        pltpu.make_async_copy(head_of(k_ref, SIDE), kv_last.at[mine, core, 0], local_sem.at[3]),
        pltpu.make_async_copy(head_of(v_ref, SIDE), kv_last.at[mine, core, 1], local_sem.at[4]),
    ]
    for copy in local:
        copy.start()
    partners = ((1, right), (3, left), (2, across_x))
    for dx, device in partners:
        send(head_of(q_ref, (x + dx) % SIDE), q_main.at[x], q_sem.at[x], device, "block")
    for dx, device in partners:
        other = (x + dx) % SIDE
        send(head_of(k_ref, other), kv_main.at[mine, core, 0], main_sem.at[mine], device, "block")
        send(head_of(v_ref, other), kv_main.at[mine, core, 1], main_sem.at[mine], device, "block")
    for copy in local:
        copy.wait()

    def pass_main(f, device):
        send(kv_main.at[f, core], kv_main.at[f, core], main_sem.at[f], device)

    def pass_last(f, device):
        send(kv_last.at[f, core], kv_last.at[f, core], last_sem.at[f], device)

    def share(ref, f, sems):
        send(ref.at[f, core], ref.at[f, core], sems.at[f], pair)

    pass_last(mine, up)
    pass_last(mine, down)
    pass_last(mine, right)
    pass_last(mine, left)
    pass_main(mine, up)
    pass_main(mine, down)
    pass_last(mine, across_y)
    share(kv_main, mine, main_pair_sem)
    share(kv_last, mine, last_pair_sem)

    query_row = lax.broadcasted_iota(jnp.int32, (tokens, 2 * tokens), 0) // 80 + core * (tokens // 80)
    key_row = lax.broadcasted_iota(jnp.int32, (tokens, 2 * tokens), 1) // 80
    far[...] = jnp.abs(query_row - key_row)
    run_max[...] = jnp.full_like(run_max, MAX_START)
    run_sum[...] = jnp.zeros_like(run_sum)
    run_acc[...] = jnp.zeros_like(run_acc)

    def arrived(ref, f, sems):
        pltpu.make_async_remote_copy(
            src_ref=ref.at[f, core], dst_ref=ref.at[f, core], send_sem=send_sem.at[0], recv_sem=sems.at[f],
            device_id=pair, device_id_type=MESH,
        ).wait_recv()

    def arrived_pair(ref, f, sems):
        pltpu.make_async_remote_copy(
            src_ref=ref.at[f, 1 - core], dst_ref=ref.at[f, 1 - core], send_sem=send_sem.at[0],
            recv_sem=sems.at[f], device_id=pair, device_id_type=MESH,
        ).wait_recv()

    def main_frame(entry):
        across, along = entry
        return frame[(across % SIDE, GRAY[along])]

    def last_frame(entry):
        across, along = entry
        return frame[(GRAY[along], across % SIDE)]

    def take_main(entry):
        f = main_frame(entry)
        across, along = entry
        arrived(kv_main, f, main_sem)
        if across == 0:
            pass_main(f, up)
            pass_main(f, down)
        if across == -1 and along in PLUS:
            pass_main(f, up)
        if across == 1 and along in MINUS:
            pass_main(f, down)
        share(kv_main, f, main_pair_sem)

    def take_last(entry):
        f = last_frame(entry)
        across, along = entry
        arrived(kv_last, f, last_sem)
        if across == 0:
            pass_last(f, right)
            pass_last(f, left)
        if across == -1 and along in PLUS:
            pass_last(f, right)
        if across == 1 and along in MINUS:
            pass_last(f, left)
        share(kv_last, f, last_pair_sem)

    for dx in (1, 3, 2):
        other = (x + dx) % SIDE
        pltpu.make_async_remote_copy(
            src_ref=q_main.at[other], dst_ref=q_main.at[other], send_sem=send_sem.at[0],
            recv_sem=q_sem.at[other], device_id=pair, device_id_type=MESH,
        ).wait_recv()

    main_frames = [main_frame(entry) for entry in MAIN_ORDER]
    last_frames = [last_frame(entry) for entry in LAST_ORDER]

    def step(k, carry):
        for kk in range(16):
            @pl.when(k == kk)
            def _():
                if kk + 1 < 16:
                    take_last(LAST_ORDER[kk + 1])
                    take_main(MAIN_ORDER[kk + 1])
                arrived_pair(kv_main, main_frames[kk], main_pair_sem)
                arrived_pair(kv_last, last_frames[kk], last_pair_sem)

        f_main, f_last = pick(k, main_frames), pick(k, last_frames)

        def operands(unit):
            if unit < SIDE:
                return q_main[unit], kv_main, f_main, y * SIDE + unit
            return q_ref[:, SIDE * HD:], kv_last, f_last, mine

        def score(unit, s_ref):
            q, kv, f, qf = operands(unit)
            keys = kv[f, :, 0].reshape(2 * tokens, HD)
            s = lax.dot_general(q, keys, (((1,), (1,)), ((), ())), preferred_element_type=jnp.float32)
            s = jnp.where(far[...] <= window[qf, f], s, NEG_FILL)
            old = run_max[unit]
            new = jnp.maximum(old, jnp.max(s, axis=-1, keepdims=True))
            s_ref[...] = s
            run_max[unit] = new
            return new, jnp.exp2((old - new) * scale)

        def gather(unit, s_ref, new, factor):
            q, kv, f, qf = operands(unit)
            weights = jnp.exp2((s_ref[...] - new[:, :1]) * scale)
            part = weights[:, :HD]
            for j in range(1, 2 * tokens // HD):
                part = part + weights[:, HD * j: HD * (j + 1)]
            run_sum[unit] = run_sum[unit] * factor + part
            values = kv[f, :, 1].reshape(2 * tokens, HD)
            run_acc[unit] = run_acc[unit] * factor + jnp.dot(
                weights.astype(jnp.bfloat16), values, preferred_element_type=jnp.float32
            )

        slots = (s_even, s_odd)
        state = score(0, slots[0])
        for unit in range(SIDE + 1):
            following = score(unit + 1, slots[(unit + 1) % 2]) if unit < SIDE else None
            gather(unit, slots[unit % 2], *state)
            state = following
        return carry

    lax.fori_loop(0, 16, step, 0)
    for unit in range(SIDE + 1):
        total = jnp.sum(run_sum[unit], axis=-1, keepdims=True)
        o_ref[unit] = (run_acc[unit] / total).astype(jnp.bfloat16)

    for slot in range(counts["piece"]):
        pltpu.make_async_remote_copy(
            src_ref=kv_main.at[0, 0], dst_ref=kv_main.at[0, 0], send_sem=send_sem.at[slot],
            recv_sem=main_sem.at[0], device_id=pair, device_id_type=MESH,
        ).wait_send()
    for position in range(counts["block"]):
        pltpu.make_async_remote_copy(
            src_ref=q_main.at[0], dst_ref=q_main.at[0], send_sem=send_sem.at[N_SENDS - 1 - position],
            recv_sem=q_sem.at[0], device_id=pair, device_id_type=MESH,
        ).wait_send()


def project_kernel(
    o_ref, w_hbm, out_ref, weights, attended, sent, got, weight_sem, move_sem, o_send, o_recv, z_send, z_recv
):
    tm, z = lax.axis_index("tm"), lax.axis_index("head")
    depth = lax.axis_size("head")
    y, x = tm // SIDE, tm % SIDE
    row = {d: {"tm": y * SIDE + (x + d) % SIDE} for d in (1, 2, 3)}
    ahead, behind = {"head": (z + 1) % depth}, {"head": (z + depth - 1) % depth}
    greet([row[1], row[3], row[2], ahead, behind])

    def head_of(ref, head):
        return ref.at[:, pl.ds(pl.multiple_of(head * HD, HD), HD)]

    returns = [
        pltpu.make_async_remote_copy(
            src_ref=o_ref.at[(x + d) % SIDE], dst_ref=head_of(attended, x), send_sem=o_send.at[d],
            recv_sem=o_recv.at[x], device_id=row[d], device_id_type=MESH,
        )
        for d in (1, 3, 2)
    ]
    for copy in returns:
        copy.start()
    moves = [
        pltpu.make_async_copy(o_ref.at[x], head_of(attended, x), move_sem.at[0]),
        pltpu.make_async_copy(o_ref.at[SIDE], head_of(attended, SIDE), move_sem.at[1]),
    ]
    width = weights.shape[1]
    loads = [
        pltpu.make_async_copy(w_hbm.at[:, pl.ds(c * width, width)], weights.at[c], weight_sem.at[c])
        for c in range(depth)
    ]
    for copy in moves + loads:
        copy.start()
    for copy in moves + loads:
        copy.wait()
    for d in (1, 3, 2):
        other = (x + d) % SIDE
        pltpu.make_async_remote_copy(
            src_ref=o_ref.at[0], dst_ref=head_of(attended, other), send_sem=o_send.at[d],
            recv_sem=o_recv.at[other], device_id=row[d], device_id_type=MESH,
        ).wait_recv()

    half = attended.shape[0] // 2
    longest = depth // 2

    def share(part, owner):
        return jnp.dot(
            attended[part * half: (part + 1) * half, :], weights[owner], preferred_element_type=jnp.float32
        )

    def hop(way, part, t):
        return pltpu.make_async_remote_copy(
            src_ref=sent.at[way, part, t], dst_ref=got.at[way, part, t], send_sem=z_send.at[way, part, t],
            recv_sem=z_recv.at[way, part, t], device_id=(ahead, behind)[way], device_id_type=MESH,
        )

    length = {(0, 0): longest, (1, 1): longest, (0, 1): longest - 1, (1, 0): longest - 1}
    for t in range(longest):
        for way, part in ((0, 0), (1, 1), (0, 1), (1, 0)):
            reach = length[(way, part)] - t
            if reach <= 0:
                continue
            owner = (z + (reach if way == 0 else depth - reach)) % depth
            total = share(part, owner)
            if t:
                hop(way, part, t - 1).wait_recv()
                total = total + got[way, part, t - 1].astype(jnp.float32)
            sent[way, part, t] = total.astype(jnp.bfloat16)
            hop(way, part, t).start()
    for part in range(2):
        total = share(part, z)
        for way in range(2):
            t = length[(way, part)] - 1
            hop(way, part, t).wait_recv()
            total = total + got[way, part, t].astype(jnp.float32)
        out_ref[part * half: (part + 1) * half, :] = total.astype(jnp.bfloat16)
    for copy in returns:
        copy.wait_send()
    for (way, part), steps in length.items():
        for t in range(steps):
            hop(way, part, t).wait_send()


def body(query, key, value, window, out_weight):
    frames_dev, rows_dev, width, feats = query.shape
    tokens = frames_dev * rows_dev * width
    units = feats // HD
    depth = lax.axis_size("head")
    f32, bf16 = jnp.float32, jnp.bfloat16
    vmem, dma = pltpu.VMEM, pltpu.SemaphoreType.DMA
    in_vmem = pl.BlockSpec(memory_space=pltpu.VMEM)
    attended = pl.pallas_call(
        attend_kernel,
        out_shape=jax.ShapeDtypeStruct((units, tokens, HD), bf16),
        in_specs=[pl.BlockSpec(memory_space=pltpu.SMEM)] + [in_vmem] * 3,
        out_specs=in_vmem,
        scratch_shapes=[
            vmem((16, 2, 2, tokens, HD), bf16),
            vmem((16, 2, 2, tokens, HD), bf16),
            vmem((SIDE, tokens, HD), bf16),
            vmem((tokens, 2 * tokens), jnp.int32),
            vmem((tokens, 2 * tokens), f32),
            vmem((tokens, 2 * tokens), f32),
            vmem((units, tokens, HD), f32),
            vmem((units, tokens, HD), f32),
            vmem((units, tokens, HD), f32),
            dma((N_SENDS,)), dma((16,)), dma((16,)), dma((16,)), dma((16,)), dma((SIDE,)), dma((5,)),
        ],
        compiler_params=pltpu.CompilerParams(
            collective_id=0, has_side_effects=True, vmem_limit_bytes=40 * 2**20
        ),
        name="attend",
    )(window, *(a.reshape(tokens, feats) for a in (query, key, value)))
    share = out_weight.shape[1] // depth
    projected = pl.pallas_call(
        project_kernel,
        out_shape=jax.ShapeDtypeStruct((tokens, share), bf16),
        in_specs=[in_vmem, pl.BlockSpec(memory_space=pl.ANY)],
        out_specs=in_vmem,
        scratch_shapes=[
            vmem((depth, feats, share), bf16),
            vmem((tokens, feats), bf16),
            vmem((2, 2, depth // 2, tokens // 2, share), bf16),
            vmem((2, 2, depth // 2, tokens // 2, share), bf16),
            dma((depth,)), dma((2,)), dma((SIDE,)), dma((SIDE,)),
            dma((2, 2, depth // 2)), dma((2, 2, depth // 2)),
        ],
        compiler_params=pltpu.CompilerParams(
            collective_id=1, has_side_effects=True, vmem_limit_bytes=40 * 2**20
        ),
        name="project",
    )(attended, out_weight)
    return projected.reshape(frames_dev, rows_dev, width, share)


def solution(mesh):
    placed = (
        P("tm", "space", None, "head"),
        P("tm", "space", None, "head"),
        P("tm", "space", None, "head"),
        P(),
        P("head", None),
    )
    return jax.shard_map(
        body, mesh=mesh, in_specs=placed, out_specs=P("tm", "space", None, "head"), check_vma=False
    )
```

```python
import math

import jax
import jax.numpy as jnp
from jax import lax
from jax.experimental import pallas as pl
from jax.experimental.pallas import tpu as pltpu
from jax.sharding import PartitionSpec as P

HD = 128
SIDE = 4
ROW = 80
NEG_FILL = -1e30
MAX_START = -1e20
MESH = pl.DeviceIdType.MESH

GRAY = (0, 1, 3, 2)
PAIRS = (
    ((-1, 0), (1, 0)),
    ((0, 1), (0, 2)),
    ((-1, 1), (1, 1)),
    ((-1, 2), (1, 2)),
    ((0, 3), (2, 0)),
    ((2, 1), (-1, 3)),
    ((1, 3), (2, 2)),
)
FINAL = (2, 3)
EVENTS = {
    ("own", 3): (("main", (-1, 0)), ("main", (1, 0))),
    (0, 2): (("main", (0, 1)), ("main", (0, 2))),
    (1, 3): (("last", 1), ("main", (-1, 1)), ("main", (1, 1))),
    (2, 2): (("last", 3),),
    (2, 3): (("main", (-1, 2)), ("main", (1, 2))),
    (3, 2): (("main", (0, 3)), ("last", 2), ("main", (2, 0))),
    (4, 2): (("main", (2, 1)), ("main", (-1, 3))),
    (5, 2): (("main", (1, 3)), ("main", (2, 2))),
    (6, 2): (("main", (2, 3)),),
}
LAST_AFTER = 3
PLUS = (0, 2)
MINUS = (1, 3)
PIECES, BLOCKS = 56, 24


def pick(index, values):
    out = values[0]
    for position, value in enumerate(values[1:], 1):
        out = jnp.where(index == position, value, out)
    return out


def layer_kernel(
    window_hbm, q_hbm, k_hbm, v_hbm, w_hbm, out_ref,
    window, q_ref, k_ref, v_ref, kv_main, kv_last, q_main, q_last, far, s_even, s_odd,
    run_max, run_sum, run_acc, last_max, last_sum, last_acc, part_sent, part_got,
    o_main, weights, attended, sent, got,
    piece_sem, block_sem, main_sem, main_pair_sem, last_sem, last_pair_sem, q_sem, q_last_sem,
    part_sem, o_sem, local_sem, weight_sem, z_send, z_recv,
):
    scale = math.log2(math.e) / math.sqrt(HD)
    f32, bf16 = jnp.float32, jnp.bfloat16
    tm, core, z = lax.axis_index("tm"), lax.axis_index("space"), lax.axis_index("head")
    depth = lax.axis_size("head")
    y, x = tm // SIDE, tm % SIDE
    tokens = q_hbm.shape[0]
    frame = {
        (dy, dx): ((y + dy) % SIDE) * SIDE + (x + dx) % SIDE for dy in range(4) for dx in range(4)
    }
    column = {d: {"tm": frame[(d, 0)]} for d in (1, 2, 3)}
    row = {d: {"tm": frame[(0, d)]} for d in (1, 2, 3)}
    up, down, right, left = column[1], column[3], row[1], row[3]
    pair = {"space": 1 - core}
    ahead, behind = {"head": (z + 1) % depth}, {"head": (z + depth - 1) % depth}
    mine = frame[(0, 0)]

    def head_of(ref, head):
        return ref.at[:, pl.ds(pl.multiple_of(head * HD, HD), HD)]

    def last_head(ref):
        return ref.at[:, pl.ds(SIDE * HD, HD)]

    width = weights.shape[1]
    first = [
        (q_hbm, q_ref),
        (k_hbm, k_ref),
        (v_hbm, v_ref),
        (head_of(k_hbm, x), kv_main.at[mine, core, 0]),
        (head_of(v_hbm, x), kv_main.at[mine, core, 1]),
        (last_head(k_hbm), kv_last.at[x, core, 0]),
        (last_head(v_hbm), kv_last.at[x, core, 1]),
        (head_of(q_hbm, x), q_main.at[x]),
        (last_head(q_hbm), q_last.at[y]),
        (window_hbm, window),
    ]
    first = [pltpu.make_async_copy(a, b, local_sem.at[i]) for i, (a, b) in enumerate(first)]
    loads = [
        pltpu.make_async_copy(w_hbm.at[:, pl.ds(c * width, width)], weights.at[c], weight_sem.at[c])
        for c in range(depth)
    ]
    for copy in first + loads:
        copy.start()

    barrier = pltpu.get_barrier_semaphore()
    partners = [*column.values(), *row.values(), pair, ahead, behind]
    for partner in partners:
        pl.semaphore_signal(barrier, inc=1, device_id=partner, device_id_type=MESH)
    pl.semaphore_wait(barrier, len(partners))
    for copy in first:
        copy.wait()

    counts = {"piece": 0, "block": 0}

    def send(src, dst, recv_sem, device, kind="piece"):
        sems = piece_sem if kind == "piece" else block_sem
        pltpu.make_async_remote_copy(
            src_ref=src, dst_ref=dst, send_sem=sems.at[counts[kind]], recv_sem=recv_sem,
            device_id=device, device_id_type=MESH,
        ).start()
        counts[kind] += 1

    def arrived(ref, sem):
        pltpu.make_async_remote_copy(
            src_ref=ref, dst_ref=ref, send_sem=piece_sem.at[0], recv_sem=sem,
            device_id=pair, device_id_type=MESH,
        ).wait_recv()

    def pass_main(f, device):
        send(kv_main.at[f, core], kv_main.at[f, core], main_sem.at[f], device)

    def share_main(f):
        send(kv_main.at[f, core], kv_main.at[f, core], main_pair_sem.at[f], pair)

    def share_last(slot):
        send(kv_last.at[slot, core], kv_last.at[slot, core], last_pair_sem.at[slot], pair)

    pass_main(mine, up)
    pass_main(mine, down)
    for d in (1, 3, 2):
        send(head_of(q_ref, (x + d) % SIDE), q_main.at[x], q_sem.at[x], row[d], "block")

    def give(d):
        other = (x + d) % SIDE
        send(head_of(k_ref, other), kv_main.at[mine, core, 0], main_sem.at[mine], row[d], "block")
        send(head_of(v_ref, other), kv_main.at[mine, core, 1], main_sem.at[mine], row[d], "block")

    give(1)
    give(3)
    share_main(mine)
    for d in (1, 3, 2):
        send(q_last.at[y], q_last.at[y], q_last_sem.at[y], column[d], "block")
    send(kv_last.at[x, core], kv_last.at[x, core], last_sem.at[x], right)
    send(kv_last.at[x, core], kv_last.at[x, core], last_sem.at[x], left)
    give(2)
    share_last(x)

    query_row = lax.broadcasted_iota(jnp.int32, (tokens, 2 * tokens), 0) // ROW + core * (tokens // ROW)
    key_row = lax.broadcasted_iota(jnp.int32, (tokens, 2 * tokens), 1) // ROW
    far[...] = jnp.abs(query_row - key_row)
    for ref in (run_max, last_max):
        ref[...] = jnp.full_like(ref, MAX_START)
    for ref in (run_sum, run_acc, last_sum, last_acc):
        ref[...] = jnp.zeros_like(ref)

    def frame_of(entry):
        return frame[(entry[0] % SIDE, GRAY[entry[1]])]

    def take(event):
        kind, entry = event
        if kind == "main":
            f = frame_of(entry)
            across, along = entry
            arrived(kv_main.at[f, core], main_sem.at[f])
            if across == 0:
                pass_main(f, up)
                pass_main(f, down)
            if across == -1 and along in PLUS:
                pass_main(f, up)
            if across == 1 and along in MINUS:
                pass_main(f, down)
            share_main(f)
        else:
            slot = (x + entry) % SIDE
            arrived(kv_last.at[slot, core], last_sem.at[slot])
            if entry == 1:
                half = kv_last.at[slot, core, 1]
                send(half, half, last_sem.at[slot], left, "block")
            if entry == 3:
                half = kv_last.at[slot, core, 0]
                send(half, half, last_sem.at[slot], right, "block")
            share_last(slot)

    def paired(f):
        arrived(kv_main.at[f, 1 - core], main_pair_sem.at[f])

    def job(units, frames, hook):
        span = 2 * tokens

        def score(unit, s_ref):
            q, query_frame, top, _, _ = unit
            best = None
            for n, (kv, f, key_frame) in enumerate(frames):
                keys = kv[f, :, 0].reshape(span, HD)
                s = lax.dot_general(q[...], keys, (((1,), (1,)), ((), ())), preferred_element_type=f32)
                s = jnp.where(far[...] <= window[query_frame, key_frame], s, NEG_FILL)
                s_ref[:, n * span: (n + 1) * span] = s
                for j in range(span // HD):
                    part = s[:, HD * j: HD * (j + 1)]
                    best = part if best is None else jnp.maximum(best, part)
            old = top[...]
            new = jnp.maximum(old, jnp.max(best, axis=-1, keepdims=True))
            top[...] = new
            return new, jnp.exp2((old - new) * scale)

        def gather(unit, s_ref, new, factor):
            _, _, _, total, acc = unit
            all_weights, product = total[...] * factor, acc[...] * factor
            for n, (kv, f, _) in enumerate(frames):
                part = jnp.exp2((s_ref[:, n * span: (n + 1) * span] - new[:, :1]) * scale)
                for j in range(span // HD):
                    all_weights = all_weights + part[:, HD * j: HD * (j + 1)]
                values = kv[f, :, 1].reshape(span, HD)
                product = product + jnp.dot(part.astype(bf16), values, preferred_element_type=f32)
            total[...] = all_weights
            acc[...] = product

        slots = (s_even, s_odd)
        hook(0)
        state = score(units[0], slots[0])
        for n, unit in enumerate(units):
            following = None
            if n + 1 < len(units):
                hook(n + 1)
                following = score(units[n + 1], slots[(n + 1) % 2])
            gather(unit, slots[n % 2], *state)
            state = following

    main_units = [
        (q_main.at[u], y * SIDE + u, run_max.at[u], run_sum.at[u], run_acc.at[u]) for u in range(SIDE)
    ]
    last_units = [
        (q_last.at[u], u * SIDE + x, last_max.at[u], last_sum.at[u], last_acc.at[u]) for u in range(SIDE)
    ]

    def own_hook(unit):
        if unit == 0:
            for d in (1, 3, 2):
                other = (x + d) % SIDE
                arrived(q_main.at[other], q_sem.at[other])
            paired(mine)
        for event in EVENTS.get(("own", unit), ()):
            take(event)

    job(main_units, [(kv_main, mine, mine)], own_hook)

    firsts = [frame_of(a) for a, _ in PAIRS]
    seconds = [frame_of(b) for _, b in PAIRS]

    def step(k, carry):
        def hook(unit):
            for kk in range(len(PAIRS)):
                events = EVENTS.get((kk, unit), ())
                if unit == 0 or events:
                    @pl.when(k == kk)
                    def _():
                        for event in events:
                            take(event)
                        if unit == 0:
                            paired(firsts[kk])
                            paired(seconds[kk])

        one, two = pick(k, firsts), pick(k, seconds)
        job(main_units, [(kv_main, one, one), (kv_main, two, two)], hook)

        @pl.when(k == LAST_AFTER)
        def _():
            for d in (1, 3, 2):
                other = (y + d) % SIDE
                arrived(q_last.at[other], q_last_sem.at[other])
            for d in range(SIDE):
                slot = (x + d) % SIDE
                arrived(kv_last.at[slot, 1 - core], last_pair_sem.at[slot])
            job(last_units, [(kv_last, n, y * SIDE + n) for n in range(SIDE)], lambda unit: None)
            lane = lax.broadcasted_iota(jnp.int32, (tokens, HD), 1)
            for u in range(SIDE):
                total = jnp.sum(last_sum[u], axis=-1, keepdims=True)
                total = jnp.maximum(total, 1e-30)
                part_sent[u, 0] = (last_acc[u] / total).astype(bf16)
                level = last_max[u] * scale + jnp.log2(total)
                high = level.astype(bf16).astype(f32)
                middle = (level - high).astype(bf16).astype(f32)
                low = level - high - middle
                part_sent[u, 1] = jnp.where(lane == 0, high, jnp.where(lane == 1, middle, low)).astype(bf16)
            for d in (1, 3, 2):
                send(part_sent.at[(y + d) % SIDE], part_got.at[y], part_sem.at[y], column[d])
            copy = pltpu.make_async_copy(part_sent.at[y], part_got.at[y], local_sem.at[0])
            copy.start()
            copy.wait()

        return carry

    lax.fori_loop(0, len(PAIRS), step, 0)
    last_one = frame_of(FINAL)

    def final_hook(unit):
        if unit == 0:
            paired(last_one)

    job(main_units, [(kv_main, last_one, last_one)], final_hook)

    for u in range(SIDE):
        total = jnp.sum(run_sum[u], axis=-1, keepdims=True)
        o_main[u] = (run_acc[u] / total).astype(bf16)
    for d in (1, 3, 2):
        send(o_main.at[(x + d) % SIDE], head_of(attended, x), o_sem.at[x], row[d], "block")
    move = pltpu.make_async_copy(o_main.at[x], head_of(attended, x), local_sem.at[0])
    move.start()
    for d in (1, 3, 2):
        other = (y + d) % SIDE
        arrived(part_got.at[other], part_sem.at[other])
    levels = [
        (part_got[u, 1, :, 0:1].astype(f32) + part_got[u, 1, :, 1:2].astype(f32))
        + part_got[u, 1, :, 2:3].astype(f32)
        for u in range(SIDE)
    ]
    highest = jnp.maximum(jnp.maximum(levels[0], levels[1]), jnp.maximum(levels[2], levels[3]))
    shares = [jnp.exp2(level - highest) for level in levels]
    merged = sum(part_got[u, 0].astype(f32) * shares[u] for u in range(SIDE))
    attended[:, SIDE * HD:] = (merged / sum(shares)).astype(bf16)
    move.wait()
    for copy in loads:
        copy.wait()
    for d in (1, 3, 2):
        other = (x + d) % SIDE
        arrived(head_of(attended, other), o_sem.at[other])

    half = tokens // 2
    longest = depth // 2

    def share(part, owner):
        return jnp.dot(
            attended[part * half: (part + 1) * half, :], weights[owner], preferred_element_type=f32
        )

    def hop(way, part, t):
        return pltpu.make_async_remote_copy(
            src_ref=sent.at[way, part, t], dst_ref=got.at[way, part, t], send_sem=z_send.at[way, part, t],
            recv_sem=z_recv.at[way, part, t], device_id=(ahead, behind)[way], device_id_type=MESH,
        )

    length = {(0, 0): longest, (1, 1): longest, (0, 1): longest - 1, (1, 0): longest - 1}
    for t in range(longest):
        for way, part in ((0, 0), (1, 1), (0, 1), (1, 0)):
            reach = length[(way, part)] - t
            if reach <= 0:
                continue
            owner = (z + (reach if way == 0 else depth - reach)) % depth
            total = share(part, owner)
            if t:
                hop(way, part, t - 1).wait_recv()
                total = total + got[way, part, t - 1].astype(f32)
            sent[way, part, t] = total.astype(bf16)
            hop(way, part, t).start()
    for part in range(2):
        total = share(part, z)
        for way in range(2):
            t = length[(way, part)] - 1
            hop(way, part, t).wait_recv()
            total = total + got[way, part, t].astype(f32)
        out_ref[part * half: (part + 1) * half, :] = total.astype(bf16)

    for (way, part), steps in length.items():
        for t in range(steps):
            hop(way, part, t).wait_send()
    for kind, sems, like in (("piece", piece_sem, kv_main.at[0, 0]), ("block", block_sem, q_main.at[0])):
        for slot in range(counts[kind]):
            pltpu.make_async_remote_copy(
                src_ref=like, dst_ref=like, send_sem=sems.at[slot], recv_sem=q_sem.at[0],
                device_id=pair, device_id_type=MESH,
            ).wait_send()


def body(query, key, value, window, out_weight):
    frames_dev, rows_dev, width, feats = query.shape
    tokens = frames_dev * rows_dev * width
    depth = lax.axis_size("head")
    share = out_weight.shape[1] // depth
    f32, bf16 = jnp.float32, jnp.bfloat16
    vmem, dma = pltpu.VMEM, pltpu.SemaphoreType.DMA
    anywhere = pl.BlockSpec(memory_space=pl.ANY)
    projected = pl.pallas_call(
        layer_kernel,
        out_shape=jax.ShapeDtypeStruct((tokens, share), bf16),
        in_specs=[anywhere] * 5,
        out_specs=pl.BlockSpec(memory_space=pltpu.VMEM),
        scratch_shapes=[
            pltpu.SMEM(window.shape, jnp.int32),
            vmem((tokens, feats), bf16), vmem((tokens, feats), bf16), vmem((tokens, feats), bf16),
            vmem((SIDE * SIDE, 2, 2, tokens, HD), bf16),
            vmem((SIDE, 2, 2, tokens, HD), bf16),
            vmem((SIDE, tokens, HD), bf16),
            vmem((SIDE, tokens, HD), bf16),
            vmem((tokens, 2 * tokens), jnp.int32),
            vmem((tokens, SIDE * 2 * tokens), f32),
            vmem((tokens, SIDE * 2 * tokens), f32),
            *[vmem((SIDE, tokens, HD), f32)] * 6,
            vmem((SIDE, 2, tokens, HD), bf16),
            vmem((SIDE, 2, tokens, HD), bf16),
            vmem((SIDE, tokens, HD), bf16),
            vmem((depth, feats, share), bf16),
            vmem((tokens, feats), bf16),
            vmem((2, 2, depth // 2, tokens // 2, share), bf16),
            vmem((2, 2, depth // 2, tokens // 2, share), bf16),
            dma((PIECES,)), dma((BLOCKS,)), dma((16,)), dma((16,)), dma((SIDE,)), dma((SIDE,)),
            dma((SIDE,)), dma((SIDE,)), dma((SIDE,)), dma((SIDE,)), dma((10,)), dma((depth,)),
            dma((2, 2, depth // 2)), dma((2, 2, depth // 2)),
        ],
        compiler_params=pltpu.CompilerParams(
            collective_id=0, has_side_effects=True, vmem_limit_bytes=63 * 2**20
        ),
        name="layer",
    )(window, *(a.reshape(tokens, feats) for a in (query, key, value)), out_weight)
    return projected.reshape(frames_dev, rows_dev, width, share)


def solution(mesh):
    placed = (
        P("tm", "space", None, "head"),
        P("tm", "space", None, "head"),
        P("tm", "space", None, "head"),
        P(),
        P("head", None),
    )
    return jax.shard_map(
        body, mesh=mesh, in_specs=placed, out_specs=P("tm", "space", None, "head"), check_vma=False
    )
```
